32 devices in a mesh: seq: 16 (over z, y, core), fsdp: 2 (over x).
Axes of the slice: x: 2, y: 2, z: 4, core: 2. Of those that a mesh axis runs over, the one named last changes fastest.
Arguments:
- residual: bfloat16 [2, 1024, 1440], P('fsdp', 'seq'), may hold values from -40 to 40
- queries: bfloat16 [2, 1024, 2048], P('fsdp', 'seq'), may hold values from -64 to 64
- key_rows: bfloat16 [2, 1024, 256], P('fsdp', 'seq'), may hold values from -16 to 16
- values: bfloat16 [2, 1024, 256], P('fsdp', 'seq'), may hold values from -1 to 2
- attention_sinks: float32 [32], replicated, may hold values from 0 to 6
- out_weight: bfloat16 [2048, 1440], P('seq', 'fsdp'), may hold values from -0.125 to 0.125
- norm_gain: bfloat16 [1440], replicated, may hold values from 0.25 to 1.75
- router_weight: bfloat16 [1440, 16], replicated, may hold values from -0.15625 to 0.15625
- gate_weight: bfloat16 [1440, 23040], P(None, 'seq'), may hold values from -0.15625 to 0.15625
- up_weight: bfloat16 [1440, 23040], P(None, 'seq'), may hold values from -0.15625 to 0.15625
- down_weight: bfloat16 [23040, 1440], P('seq'), may hold values from -0.15625 to 0.15625
- routing: int32 [2, 1024, 2], P('fsdp', 'seq'), may hold values from 0 to 15, as said below
- span_order: int32 [32], replicated, may hold values from 0 to 31, as said below
Outputs:
- attended: bfloat16 [2, 1024, 1440], P('fsdp', 'seq')
- layer_output: bfloat16 [2, 1024, 1440], P('fsdp', 'seq')
The draws below stay inside these ranges and needn't reach their ends.
Inputs may be any that keep to these rules, and one draw needn't show every extreme that they name: A permutation of 0 to 31; index i of seq holds the rows of spans span_order[2 i] and span_order[2 i + 1], and these two add up to 31. `routing`: in the rows of one device no expert is named more than 12 times; in each prompt one expert is named exactly 12 times in the rows of every device; the 2 experts of a row differ.
All inputs are finite; a program needn't handle non-finite values.
Results may differ from the reference program's by a relative error of at most 0.009.
Values may be sent and summed in bfloat16 or wider, within the bound.
A program may use at most 64 MiB of HBM per device.

```python
import jax
import jax.numpy as jnp
from jax import lax

D = 1440
HEADS = 32
KVH = 4
HD = 64
EXPERTS = 16
FFE = 1440
TOPK = 2
TOK_DEV = 64
HALF = 32
CAP = 12
PROMPTS = 2
TOKENS = 1024
SPANS = 32
UNITS = 1440
N_SEQ = 16


def draw_residual(key, part):
    noise_part = jax.random.normal(jax.random.fold_in(key, 7), (PROMPTS, TOKENS, D), jnp.float32)
    return jnp.clip(noise_part, -40.0, 40.0).astype(jnp.bfloat16)


def draw_queries(key, part):
    noise_key = jax.random.fold_in(key, 3)
    drawn = jax.random.normal(noise_key, (PROMPTS, TOKENS, HEADS, HD), jnp.float32)
    return jnp.clip(drawn, -64.0, 64.0).reshape(PROMPTS, TOKENS, HEADS * HD).astype(jnp.bfloat16)


def draw_key_rows(key, part):
    noise_key = jax.random.fold_in(key, 5)
    drawn = jax.random.normal(noise_key, (PROMPTS, TOKENS, KVH, HD), jnp.float32)
    return jnp.clip(drawn, -16.0, 16.0).reshape(PROMPTS, TOKENS, KVH * HD).astype(jnp.bfloat16)


def draw_span_order(key, part):
    pair_index = jax.random.permutation(jax.random.fold_in(key, 21), SPANS // 2).astype(jnp.int32)
    flip_order = jax.random.randint(jax.random.fold_in(key, 22), (SPANS // 2,), 0, 2).astype(jnp.int32)
    first_span = jnp.where(flip_order == 1, SPANS - 1 - pair_index, pair_index)
    return jnp.stack([first_span, SPANS - 1 - first_span], axis=1).reshape(SPANS).astype(jnp.int32)


def route_block(block_key, hot_expert):
    perm_key, order_key, turn_key = jax.random.split(block_key, 3)
    spare_slots = jax.random.permutation(perm_key, (EXPERTS - 1) * CAP)[:TOK_DEV * TOPK - CAP]
    others = (jnp.sort(spare_slots) // CAP).astype(jnp.int32)
    others = others + (others >= hot_expert).astype(jnp.int32)
    listed = jnp.concatenate([jnp.full((CAP,), hot_expert, jnp.int32), others])
    table_rows = listed.reshape(TOPK, TOK_DEV).T
    table_rows = table_rows[jax.random.permutation(order_key, TOK_DEV)]
    turn_by = jax.random.randint(turn_key, (TOK_DEV, 1), 0, TOPK)
    column_order = (jnp.arange(TOPK, dtype=jnp.int32)[None, :] + turn_by) % TOPK
    return jnp.take_along_axis(table_rows, column_order, axis=1).astype(jnp.int32)


def draw_routing(key, part):
    blocks = TOKENS // TOK_DEV
    hot_experts = jax.random.randint(jax.random.fold_in(key, 31), (PROMPTS,), 0, EXPERTS).astype(jnp.int32)
    block_keys = jax.random.split(jax.random.fold_in(key, 32), PROMPTS * blocks)
    hot_each = jnp.repeat(hot_experts, blocks)
    tables = jax.vmap(route_block)(block_keys, hot_each)
    return tables.reshape(PROMPTS, TOKENS, TOPK).astype(jnp.int32)


def steps_of(own_key, dims, pieces, low, top_value):
    def one(axis_at, shards_of):
        steps = jax.random.uniform(jax.random.fold_in(jax.random.fold_in(own_key, 6), axis_at), (shards_of,), jnp.float32, low / len(pieces), top_value / len(pieces))
        return jnp.repeat(jnp.exp(steps), dims[axis_at] // shards_of).reshape((-1,) + (1,) * (len(dims) - axis_at - 1))

    level = one(*pieces[0])
    for cut in pieces[1:]:
        level = level * one(*cut)
    return level


def gaussian(stream_key, dims, scale, bound, shards=(), kind=jnp.bfloat16):
    values = jax.random.normal(stream_key, dims, jnp.float32) * scale
    if len(shards) > 0:
        values = steps_of(stream_key, dims, shards, -0.22, 0.18) * values
    return jnp.clip(values, min=-bound, max=bound).astype(kind)


def setup_inputs(seed: int = 0) -> dict:
    splits = jax.random.split(jax.random.key(seed), 14)
    residual = draw_residual(jax.random.fold_in(splits[13], 71), 0)
    queries = draw_queries(jax.random.fold_in(splits[13], 71), 0)
    key_rows = draw_key_rows(jax.random.fold_in(splits[13], 71), 0)
    values = jnp.clip(-1.0 + 3.0 * jax.random.uniform(splits[3], (PROMPTS, TOKENS, KVH * HD), jnp.float32) ** steps_of(splits[3], (PROMPTS, TOKENS, KVH * HD), ((0, 2), (1, 16)), -0.2, 0.2), -1.0, 2.0).astype(jnp.bfloat16)
    attention_sinks = jnp.clip(jax.random.uniform(splits[4], (HEADS,), jnp.float32, 0.0, 6.0), 0.0, 6.0)
    out_weight = gaussian(splits[5], (HEADS * HD, D), (HEADS * HD) ** -0.5, 0.125, ((0, 16), (1, 2)))
    norm_gain = jnp.clip(1.0 + 0.15 * jax.random.normal(splits[6], (D,), jnp.float32), 0.25, 1.75).astype(jnp.bfloat16)
    router_weight = gaussian(splits[7], (D, EXPERTS), D ** -0.5, 0.15625)
    gate_weight = gaussian(splits[8], (D, EXPERTS * FFE), D ** -0.5, 0.15625, ((1, 16),))
    up_weight = gaussian(splits[9], (D, EXPERTS * FFE), D ** -0.5, 0.15625, ((1, 16),))
    down_weight = gaussian(splits[10], (EXPERTS * FFE, D), FFE ** -0.5, 0.15625, ((0, 16),))
    routing = draw_routing(jax.random.fold_in(splits[13], 71), 0)
    span_order = draw_span_order(jax.random.fold_in(splits[13], 71), 0)
    return dict(residual=residual, queries=queries, key_rows=key_rows, values=values, attention_sinks=attention_sinks, out_weight=out_weight, norm_gain=norm_gain, router_weight=router_weight, gate_weight=gate_weight, up_weight=up_weight, down_weight=down_weight, routing=routing, span_order=span_order)


rope_base = 150000.0
norm_eps = 1e-05
masked_score = -1e+30

def lookup(table_values, lookup_index):
    matches = lookup_index[:, None] == jnp.arange(table_values.shape[0], dtype=jnp.int32)[None, :]
    return lax.optimization_barrier(jnp.sum(jnp.where(matches, table_values[None, :], 0), axis=1)).astype(jnp.int32)

def positions(span_order, row_index):
    device = row_index // TOK_DEV
    within = row_index % TOK_DEV
    span_index = lookup(span_order, 2 * device + within // HALF)
    return span_index * HALF + within % HALF

def rotate(head_values, where_at):
    half_size = head_values.shape[-1] // 2
    frequency = jnp.exp(-jnp.log(rope_base) * jnp.arange(half_size, dtype=jnp.float32) / half_size)
    angles = where_at.astype(jnp.float32)[:, None] * frequency[None, :]
    cosine = jnp.cos(angles)[:, None, :]
    sine_part = jnp.sin(angles)[:, None, :]
    first_half = head_values[..., :half_size]
    second = head_values[..., half_size:]
    return jnp.concatenate([first_half * cosine - second * sine_part, second * cosine + first_half * sine_part], axis=-1)

def slot_of(chosen):
    flattened = chosen.reshape(-1)
    onehot = (flattened[:, None] == jnp.arange(EXPERTS, dtype=jnp.int32)[None, :]).astype(jnp.int32)
    before = jnp.cumsum(onehot, axis=0) - onehot
    return lax.optimization_barrier(jnp.sum(before * onehot, axis=1)).reshape(chosen.shape).astype(jnp.int32)

def reference(residual, queries, key_rows, values, attention_sinks, out_weight, norm_gain, router_weight, gate_weight, up_weight, down_weight, routing, span_order):
    where_at = positions(span_order, jnp.arange(TOKENS, dtype=jnp.int32))
    visible = where_at[None, :] <= where_at[:, None]
    score_scale = HD ** (-0.5)
    group_size = HEADS // KVH

    def attend_prompt(operands):
        query_prompt, key_prompt, value_prompt = operands
        query_rot = rotate(query_prompt.astype(jnp.float32).reshape(TOKENS, HEADS, HD), where_at).astype(jnp.bfloat16)
        key_rot = rotate(key_prompt.astype(jnp.float32).reshape(TOKENS, KVH, HD), where_at).astype(jnp.bfloat16)
        value_heads = value_prompt.reshape(TOKENS, KVH, HD)

        def attend_head(head_index):
            group_index = head_index // group_size
            query_one = lax.dynamic_index_in_dim(query_rot, head_index, 1, keepdims=False).astype(jnp.float32)
            key_one = lax.dynamic_index_in_dim(key_rot, group_index, 1, keepdims=False).astype(jnp.float32)
            value_one = lax.dynamic_index_in_dim(value_heads, group_index, 1, keepdims=False)
            sink_one = lax.dynamic_index_in_dim(attention_sinks, head_index, 0, keepdims=False).astype(jnp.float32)
            scores = jnp.dot(query_one, key_one.T, preferred_element_type=jnp.float32, precision=lax.Precision.HIGHEST) * score_scale
            scores = jnp.where(visible, scores, masked_score)
            row_max = jnp.maximum(lax.optimization_barrier(jnp.max(scores, axis=1)), sink_one)
            weight = jnp.exp(scores - row_max[:, None])
            denominator = lax.optimization_barrier(jnp.sum(weight, axis=1)) + jnp.exp(sink_one - row_max)
            weighted = jnp.dot(weight.astype(jnp.bfloat16), value_one, preferred_element_type=jnp.float32)
            return weighted / denominator[:, None]
        heads_out = lax.map(attend_head, jnp.arange(HEADS, dtype=jnp.int32))
        return jnp.transpose(heads_out, (1, 0, 2)).reshape(TOKENS, HEADS * HD).astype(jnp.bfloat16)
    attention_rows = lax.map(attend_prompt, (queries, key_rows, values))
    attended = jnp.dot(attention_rows.reshape(PROMPTS * TOKENS, HEADS * HD), out_weight, preferred_element_type=jnp.float32).astype(jnp.bfloat16)
    attended = attended.reshape(PROMPTS, TOKENS, D)
    stream = residual.astype(jnp.float32) + attended.astype(jnp.float32)
    normed = (stream * lax.rsqrt(lax.optimization_barrier(jnp.mean(stream * stream, axis=-1, keepdims=True)) + norm_eps) * norm_gain.astype(jnp.float32)).astype(jnp.bfloat16)
    logits = jnp.dot(normed.reshape(PROMPTS * TOKENS, D), router_weight, preferred_element_type=jnp.float32).reshape(PROMPTS, TOKENS, EXPERTS)
    selected = jnp.take_along_axis(logits, routing, axis=-1)
    gates = 1.0 / lax.optimization_barrier(jnp.sum(jnp.exp(selected[..., :, None] - selected[..., None, :]), axis=-2))

    def expert_prompt(operands):
        normed_prompt, chosen_prompt, gates_prompt = operands
        blocks_in = normed_prompt.reshape(N_SEQ, TOK_DEV, D)
        chosen_blocks = chosen_prompt.reshape(N_SEQ, TOK_DEV, TOPK)
        slot_blocks = jax.vmap(slot_of)(chosen_blocks)
        target = chosen_blocks * CAP + slot_blocks

        def dispatch_one(target_block, rows_block):
            mapping = lax.optimization_barrier(jnp.sum((target_block[None, :, :] == jnp.arange(EXPERTS * CAP, dtype=jnp.int32)[:, None, None]).astype(jnp.int32), axis=2))
            return jnp.dot(mapping.astype(jnp.bfloat16), rows_block, preferred_element_type=jnp.float32).astype(jnp.bfloat16)
        buffers = jax.vmap(dispatch_one)(target, blocks_in).reshape(N_SEQ, EXPERTS, CAP, D)

        def run_one(expert_index):
            expert_rows = lax.dynamic_index_in_dim(buffers, expert_index, 1, keepdims=False).reshape(N_SEQ * CAP, D)
            gate_columns = lax.dynamic_slice_in_dim(gate_weight, (expert_index * FFE).astype(jnp.int32), FFE, 1)
            up_columns = lax.dynamic_slice_in_dim(up_weight, (expert_index * FFE).astype(jnp.int32), FFE, 1)
            down_rows = lax.dynamic_slice_in_dim(down_weight, (expert_index * FFE).astype(jnp.int32), FFE, 0)
            gate_values = jnp.dot(expert_rows, gate_columns, preferred_element_type=jnp.float32)
            up_values = jnp.dot(expert_rows, up_columns, preferred_element_type=jnp.float32)
            hidden = (gate_values * jax.nn.sigmoid(1.702 * gate_values) * (up_values + 1.0)).astype(jnp.bfloat16)
            parts = jnp.einsum('rgu,gud->rgd', hidden.reshape(N_SEQ * CAP, FFE // UNITS, UNITS).astype(jnp.float32), down_rows.reshape(FFE // UNITS, UNITS, D).astype(jnp.float32))
            rounded = lax.optimization_barrier(parts.astype(jnp.bfloat16))
            return lax.optimization_barrier(jnp.sum(rounded.astype(jnp.float32), axis=1))
        outputs = lax.map(run_one, jnp.arange(EXPERTS, dtype=jnp.int32)).reshape(EXPERTS * N_SEQ * CAP, D)
        device_index = jnp.arange(N_SEQ, dtype=jnp.int32)[:, None, None]
        flat_index = ((chosen_blocks * N_SEQ + device_index) * CAP + slot_blocks).reshape(-1).astype(jnp.int32)
        chosen_out = jnp.take(outputs, flat_index, axis=0).reshape(TOKENS, TOPK, D)
        return lax.optimization_barrier(jnp.sum(chosen_out * gates_prompt[:, :, None], axis=1))
    expert_mix = lax.map(expert_prompt, (normed, routing, gates))
    layer_output = (stream + expert_mix).astype(jnp.bfloat16)
    return (attended, layer_output)
```

```python
import functools

import jax
import jax.numpy as jnp
from jax import lax
from jax.experimental import pallas as pl
from jax.experimental.pallas import tpu as pltpu
from jax.sharding import PartitionSpec as P

D = 1440
HEADS = 32
KVH = 4
HD = 64
EXPERTS = 16
TOPK = 2
TOK_DEV = 64
HALF = 32
CAP = 12


rope_base = 150000.0
norm_eps = 1e-05
masked_score = -1e30
block_rows = 512


def lookup(table_values, lookup_index):
    matches = lookup_index[:, None] == jnp.arange(table_values.shape[0], dtype=jnp.int32)[None, :]
    return jnp.sum(jnp.where(matches, table_values[None, :], 0), axis=1)


def positions(span_order, row_index):
    device = row_index // TOK_DEV
    within = row_index % TOK_DEV
    span_index = lookup(span_order, 2 * device + within // HALF)
    return span_index * HALF + within % HALF


def rotate(head_values, where_at):
    half_size = head_values.shape[-1] // 2
    frequency = jnp.exp(-jnp.log(rope_base) * jnp.arange(half_size, dtype=jnp.float32) / half_size)
    angles = where_at.astype(jnp.float32)[:, None] * frequency[None, :]
    cosine = jnp.cos(angles)[:, None, :]
    sine_part = jnp.sin(angles)[:, None, :]
    first_half = head_values[..., :half_size]
    second = head_values[..., half_size:]
    return jnp.concatenate(
        [first_half * cosine - second * sine_part, second * cosine + first_half * sine_part],
        axis=-1,
    )


def slot_of(chosen):
    flattened = chosen.reshape(-1)
    onehot = (flattened[:, None] == jnp.arange(EXPERTS, dtype=jnp.int32)[None, :]).astype(jnp.int32)
    before = jnp.cumsum(onehot, axis=0) - onehot
    return jnp.sum(before * onehot, axis=1).reshape(chosen.shape)


MESH = pl.DeviceIdType.MESH


def remote(source, target, send_sem, recv_sem, **where):
    return pltpu.make_async_remote_copy(
        src_ref=source,
        dst_ref=target,
        send_sem=send_sem,
        recv_sem=recv_sem,
        device_id=where,
        device_id_type=MESH,
    )


def greet(peers):
    barrier = pltpu.get_barrier_semaphore()
    for where in peers:
        pl.semaphore_signal(barrier, inc=1, device_id=where, device_id_type=MESH)
    pl.semaphore_wait(barrier, len(peers))


def gather_plan(block, slots, sems, z_count, z, y, c):
    z_send, z_recv, y_send, y_recv, c_send, c_recv, own_sem = sems

    def slot(zz, yy, cc):
        return (zz * 2 + yy) * 2 + cc

    def z_of(d):
        return lax.rem(z + z_count - d, z_count)

    own = slot(z, y, c)
    to_z = [
        remote(block, slots.at[own], z_send.at[d], z_recv.at[d], seq=slot(lax.rem(z + d, z_count), y, c))
        for d in range(1, z_count)
    ]

    def to_y(d):
        source = block if d == 0 else slots.at[slot(z_of(d), y, c)]
        return remote(source, slots.at[slot(z_of(d), y, c)], y_send.at[d], y_recv.at[d], seq=slot(z, 1 - y, c))

    def to_c(side, d):
        index = slot(z_of(d), y if side == 0 else 1 - y, c)
        source = block if side == 0 and d == 0 else slots.at[index]
        return remote(source, slots.at[index], c_send.at[side, d], c_recv.at[side, d], seq=slot(z, y, 1 - c))

    local = pltpu.make_async_copy(block, slots.at[own], own_sem)
    ys = [to_y(d) for d in range(z_count)]
    cs = [[to_c(side, d) for d in range(z_count)] for side in range(2)]

    def start_z():
        local.start()
        for copy in to_z:
            copy.start()

    def relay(d):
        if d > 0:
            to_z[d - 1].wait_recv()
        ys[d].start()
        cs[0][d].start()

    def relay_across(d):
        ys[d].wait_recv()
        cs[1][d].start()

    def finish():
        for side in range(2):
            for d in range(z_count):
                cs[side][d].wait_recv()
        local.wait()

    def drain():
        for copy in to_z + ys + cs[0] + cs[1]:
            copy.wait_send()

    return start_z, relay, relay_across, finish, drain


def attend_kernel(
    seq_count, fsdp_count,
    q_ref, kv_ref, w_ref, qpos_ref, kpos_ref, sink_ref,
    out_ref,
    kv_all, w_all, bias, rows_all, proj, got,
    kzs, kzr, kys, kyr, kcs, kcr, wzs, wzr, wys, wyr, wcs, wcr, own_sems, as_, ar, ps, pr,
):
    me = lax.axis_index("seq")
    f_me = lax.axis_index("fsdp")
    z_count = seq_count // 4
    z, y, c = me // 4, lax.rem(me // 2, 2), lax.rem(me, 2)
    peers = [{"seq": (lax.rem(z + d, z_count) * 2 + y) * 2 + c} for d in range(1, z_count)]
    peers += [{"seq": (z * 2 + 1 - y) * 2 + c}, {"seq": (z * 2 + y) * 2 + 1 - c}]
    peers += [{"fsdp": lax.rem(f_me + d, fsdp_count)} for d in range(1, fsdp_count)]
    greet(peers)

    kv = gather_plan(kv_ref, kv_all, (kzs, kzr, kys, kyr, kcs, kcr, own_sems.at[0]), z_count, z, y, c)
    w = gather_plan(w_ref, w_all, (wzs, wzr, wys, wyr, wcs, wcr, own_sems.at[1]), z_count, z, y, c)
    kv[0]()
    for d in range(z_count):
        kv[1](d)
    w[0]()
    bias[...] = jnp.where(kpos_ref[...] <= qpos_ref[...], 0.0, masked_score)
    for d in range(z_count):
        kv[2](d)
    w[1](0)
    kv[3]()

    rows, key_count = bias.shape
    group_size = HEADS // KVH
    chunk = 4
    pending = [("z", d) for d in range(1, z_count)] + [("y", d) for d in range(z_count)]
    steps = KVH * (group_size // chunk)
    per_step = -(-len(pending) // steps)

    def send_rows(g):
        return [
            remote(
                rows_all.at[g, f_me], rows_all.at[g, f_me], as_.at[g, d], ar.at[g, d],
                fsdp=lax.rem(f_me + d, fsdp_count),
            )
            for d in range(1, fsdp_count)
        ]

    row_copies = [send_rows(g) for g in range(KVH)]
    for g in range(KVH):
        keys = kv_all[:, :, g * HD:(g + 1) * HD].reshape(key_count, HD)
        vals = kv_all[:, :, (KVH + g) * HD:(KVH + g + 1) * HD].reshape(key_count, HD)
        parts = []
        for part in range(group_size // chunk):
            q = q_ref[g, part * chunk * rows:(part + 1) * chunk * rows, :]
            s = lax.dot_general(q, keys, (((1,), (1,)), ((), ())), preferred_element_type=jnp.float32)
            weights, totals = [], []
            for i in range(chunk):
                sink = sink_ref[0, g * group_size + part * chunk + i]
                one = s[i * rows:(i + 1) * rows, :] + bias[...]
                top = jnp.maximum(jnp.max(one, axis=1, keepdims=True), sink)
                p = jnp.exp(one - top)
                totals.append(jnp.sum(p, axis=1, keepdims=True) + jnp.exp(sink - top))
                weights.append(p.astype(jnp.bfloat16))
            o = jnp.dot(jnp.concatenate(weights, axis=0), vals, preferred_element_type=jnp.float32)
            for i in range(chunk):
                parts.append((o[i * rows:(i + 1) * rows, :] / totals[i]).astype(jnp.bfloat16))
            if part == 0 and g > 0:
                for copy in row_copies[g - 1]:
                    copy.start()
        rows_all[g, pl.ds(f_me, 1)] = jnp.concatenate(parts, axis=1)[None]
    for kind, d in pending:
        w[1](d) if kind == "z" else w[2](d)
    for copy in row_copies[KVH - 1]:
        copy.start()
    w[3]()

    width = group_size * HD
    per = w_ref.shape[0]
    count = width // per
    total = None
    for g in range(KVH):
        for copy in row_copies[g]:
            copy.wait_recv()
        block = w_all[g * count:(g + 1) * count].reshape(width, w_ref.shape[1])
        term = jnp.dot(
            rows_all[g].reshape(fsdp_count * rows, width), block, preferred_element_type=jnp.float32
        )
        total = term if total is None else total + term
    proj[...] = total.astype(jnp.bfloat16).reshape(proj.shape)
    backs = []
    for d in range(1, fsdp_count):
        peer = lax.rem(f_me + d, fsdp_count)
        backs.append(remote(proj.at[peer], got.at[f_me], ps.at[d], pr.at[d], fsdp=peer))
    for copy in backs:
        copy.start()
    got[pl.ds(f_me, 1)] = proj[pl.ds(f_me, 1)]
    kv[4]()
    w[4]()
    for g in range(KVH):
        for copy in row_copies[g]:
            copy.wait_send()
    for copy in backs:
        copy.wait_recv()
    out_ref[...] = got[...]
    for copy in backs:
        copy.wait_send()


def attend(seq_count, fsdp_count, q, kv, w, qpos, kpos, sinks):
    rows = kv.shape[0]
    z_count = seq_count // 4
    dma = pltpu.SemaphoreType.DMA
    vmem = pl.BlockSpec(memory_space=pltpu.VMEM)
    gather_sems = [dma((z_count,))] * 4 + [dma((2, z_count))] * 2
    return pl.pallas_call(
        functools.partial(attend_kernel, seq_count, fsdp_count),
        out_shape=jax.ShapeDtypeStruct((fsdp_count, rows, w.shape[1]), jnp.bfloat16),
        in_specs=[vmem] * 5 + [pl.BlockSpec(memory_space=pltpu.SMEM)],
        out_specs=vmem,
        scratch_shapes=[
            pltpu.VMEM((seq_count,) + kv.shape, jnp.bfloat16),
            pltpu.VMEM((seq_count,) + w.shape, jnp.bfloat16),
            pltpu.VMEM((rows, seq_count * rows), jnp.float32),
            pltpu.VMEM((KVH, fsdp_count, rows, HEADS // KVH * HD), jnp.bfloat16),
            pltpu.VMEM((fsdp_count, rows, w.shape[1]), jnp.bfloat16),
            pltpu.VMEM((fsdp_count, rows, w.shape[1]), jnp.bfloat16),
        ]
        + gather_sems
        + gather_sems
        + [dma((2,)), dma((KVH, fsdp_count)), dma((KVH, fsdp_count)), dma((fsdp_count,)), dma((fsdp_count,))],
        compiler_params=pltpu.CompilerParams(
            collective_id=0, has_side_effects=True, vmem_limit_bytes=60 * 1024 * 1024
        ),
    )(q, kv, w, qpos, kpos, sinks)


def expert_kernel(
    seq_count, copies,
    x_ref, gate_hbm, up_hbm, down_hbm,
    out_ref,
    gate, up, down, arrived, stacked, back, load_sems, xs, xr, bs, br, own_sems,
):
    loads = [
        pltpu.make_async_copy(source, target, load_sems.at[i])
        for i, (source, target) in enumerate(((gate_hbm, gate), (up_hbm, up), (down_hbm, down)))
    ]
    for load in loads:
        load.start()
    me = lax.axis_index("seq")
    greet([{"seq": lax.rem(me + d, seq_count)} for d in range(1, seq_count)])
    sends = []
    for d in range(1, seq_count):
        peer = lax.rem(me + d, seq_count)
        sends.append(remote(x_ref.at[peer // copies], arrived.at[me], xs.at[d], xr.at[d], seq=peer))
    own = pltpu.make_async_copy(x_ref.at[me // copies], arrived.at[me], own_sems.at[0])
    for copy in sends:
        copy.start()
    own.start()
    for copy in sends:
        copy.wait_recv()
    own.wait()
    for i in range(seq_count):
        stacked[i * CAP:(i + 1) * CAP, :] = arrived[i]
    for load in loads:
        load.wait()
    x = stacked[...]
    g = jnp.dot(x, gate[...], preferred_element_type=jnp.float32)
    u = jnp.dot(x, up[...], preferred_element_type=jnp.float32)
    hidden = (g * jax.nn.sigmoid(1.702 * g) * (u + 1.0)).astype(jnp.bfloat16)
    part = jnp.dot(hidden, down[...], preferred_element_type=jnp.float32).astype(jnp.bfloat16)
    for i in range(seq_count):
        back[i] = part[i * CAP:(i + 1) * CAP, :]
    returns = []
    for d in range(1, seq_count):
        peer = lax.rem(me + d, seq_count)
        returns.append(remote(back.at[peer], out_ref.at[me], bs.at[d], br.at[d], seq=peer))
    keep = pltpu.make_async_copy(back.at[me], out_ref.at[me], own_sems.at[1])
    for copy in returns:
        copy.start()
    keep.start()
    for copy in sends:
        copy.wait_send()
    for copy in returns:
        copy.wait_recv()
    keep.wait()
    for copy in returns:
        copy.wait_send()


def run_experts(seq_count, copies, x, gate_weight, up_weight, down_weight):
    dma = pltpu.SemaphoreType.DMA
    vmem = pl.BlockSpec(memory_space=pltpu.VMEM)
    hbm = pl.BlockSpec(memory_space=pl.ANY)
    cap, width = x.shape[1:]
    return pl.pallas_call(
        functools.partial(expert_kernel, seq_count, copies),
        out_shape=jax.ShapeDtypeStruct((seq_count, cap, width), jnp.bfloat16),
        in_specs=[vmem] + [hbm] * 3,
        out_specs=vmem,
        scratch_shapes=[
            pltpu.VMEM(gate_weight.shape, jnp.bfloat16),
            pltpu.VMEM(up_weight.shape, jnp.bfloat16),
            pltpu.VMEM(down_weight.shape, jnp.bfloat16),
            pltpu.VMEM((seq_count, cap, width), jnp.bfloat16),
            pltpu.VMEM((seq_count * cap, width), jnp.bfloat16),
            pltpu.VMEM((seq_count, cap, width), jnp.bfloat16),
            dma((3,)),
            dma((seq_count,)),
            dma((seq_count,)),
            dma((seq_count,)),
            dma((seq_count,)),
            dma((2,)),
        ],
        compiler_params=pltpu.CompilerParams(
            collective_id=1, has_side_effects=True, vmem_limit_bytes=60 * 1024 * 1024
        ),
    )(x, gate_weight, up_weight, down_weight)


def on_device(
    residual,
    queries,
    key_rows,
    values,
    attention_sinks,
    out_weight,
    norm_gain,
    router_weight,
    gate_weight,
    up_weight,
    down_weight,
    routing,
    span_order,
):
    seq_count = lax.axis_size("seq")
    seq_index = lax.axis_index("seq")
    token_count = residual.shape[1]
    group_size = HEADS // KVH
    score_scale = HD ** (-0.5)
    query_at = positions(
        span_order, seq_index * token_count + jnp.arange(token_count, dtype=jnp.int32)
    )
    query_rot = rotate(
        queries[0].astype(jnp.float32).reshape(token_count, HEADS, HD), query_at
    ).astype(jnp.bfloat16)
    query_rot = (query_rot * score_scale).reshape(token_count, KVH, group_size, HD)
    query_rot = query_rot.transpose(1, 2, 0, 3).reshape(KVH, group_size * token_count, HD)
    key_rot = rotate(
        key_rows[0].astype(jnp.float32).reshape(token_count, KVH, HD), query_at
    ).astype(jnp.bfloat16)
    key_rot = key_rot.reshape(token_count, KVH * HD)
    kv = jnp.concatenate([key_rot, values[0]], axis=1)
    key_at = positions(span_order, jnp.arange(seq_count * token_count, dtype=jnp.int32))
    blocks = attend(
        seq_count,
        lax.axis_size("fsdp"),
        query_rot,
        kv,
        out_weight,
        query_at[:, None],
        key_at[None, :],
        attention_sinks[None, :],
    )
    attended = jnp.transpose(blocks, (1, 0, 2)).reshape(token_count, D)
    stream = residual[0].astype(jnp.float32) + attended.astype(jnp.float32)
    normed = (
        stream
        * lax.rsqrt(jnp.mean(stream * stream, axis=-1, keepdims=True) + norm_eps)
        * norm_gain.astype(jnp.float32)
    ).astype(jnp.bfloat16)
    logits = jnp.dot(normed, router_weight, preferred_element_type=jnp.float32)
    chosen = routing[0]
    matches = chosen[:, :, None] == jnp.arange(EXPERTS, dtype=jnp.int32)[None, None, :]
    chosen_logits = jnp.sum(jnp.where(matches, logits[:, None, :], 0.0), axis=-1)
    gates = 1.0 / jnp.sum(jnp.exp(chosen_logits[:, :, None] - chosen_logits[:, None, :]), axis=1)
    slot_index = slot_of(chosen)
    target = chosen * CAP + slot_index
    dispatch_map = jnp.sum(
        (target[None, :, :] == jnp.arange(EXPERTS * CAP, dtype=jnp.int32)[:, None, None]).astype(
            jnp.int32
        ),
        axis=2,
    )
    buffer = jnp.dot(
        dispatch_map.astype(jnp.bfloat16), normed, preferred_element_type=jnp.float32
    ).astype(jnp.bfloat16)
    copies = seq_count // EXPERTS
    returned = run_experts(
        seq_count,
        copies,
        buffer.reshape(EXPERTS, CAP, D),
        gate_weight,
        up_weight,
        down_weight,
    )
    summed = jnp.sum(returned.reshape(EXPERTS, copies, CAP, D).astype(jnp.float32), axis=1).reshape(
        EXPERTS * CAP, D
    )
    chosen_out = jnp.take(summed, target.reshape(-1), axis=0).reshape(token_count, TOPK, D)
    expert_mix = jnp.sum(chosen_out * gates[:, :, None], axis=1)
    layer_output = (stream + expert_mix).astype(jnp.bfloat16)
    return (attended[None], layer_output[None])


def solution(mesh):
    in_specs = (
        P("fsdp", "seq", None),
        P("fsdp", "seq", None),
        P("fsdp", "seq", None),
        P("fsdp", "seq", None),
        P(),
        P("seq", "fsdp"),
        P(),
        P(),
        P(None, "seq"),
        P(None, "seq"),
        P("seq", None),
        P("fsdp", "seq", None),
        P(),
    )
    out_specs = (P("fsdp", "seq", None), P("fsdp", "seq", None))
    return jax.shard_map(
        on_device, mesh=mesh, in_specs=in_specs, out_specs=out_specs, check_vma=False
    )
```

```python
import functools

import jax
import jax.numpy as jnp
from jax import lax
from jax.experimental import pallas as pl
from jax.experimental.pallas import tpu as pltpu
from jax.sharding import PartitionSpec as P

D = 1440
HEADS = 32
KVH = 4
HD = 64
EXPERTS = 16
TOPK = 2
TOK_DEV = 64
HALF = 32
CAP = 12


rope_base = 150000.0
norm_eps = 1e-05
masked_score = -1e30


MESH = pl.DeviceIdType.MESH


def remote(source, target, send_sem, recv_sem, **where):
    return pltpu.make_async_remote_copy(
        src_ref=source,
        dst_ref=target,
        send_sem=send_sem,
        recv_sem=recv_sem,
        device_id=where,
        device_id_type=MESH,
    )


def greet(peers):
    barrier = pltpu.get_barrier_semaphore()
    for where in peers:
        pl.semaphore_signal(barrier, inc=1, device_id=where, device_id_type=MESH)
    pl.semaphore_wait(barrier, len(peers))


def gather_plan(block, slots, sems, z_count, z, y, c):
    z_send, z_recv, y_send, y_recv, c_send, c_recv, own_sem = sems

    def slot(zz, yy, cc):
        return (zz * 2 + yy) * 2 + cc

    def z_of(d):
        return lax.rem(z + z_count - d, z_count)

    own = slot(z, y, c)
    to_z = [
        remote(block, slots.at[own], z_send.at[d], z_recv.at[d], seq=slot(lax.rem(z + d, z_count), y, c))
        for d in range(1, z_count)
    ]

    def to_y(d):
        source = block if d == 0 else slots.at[slot(z_of(d), y, c)]
        return remote(source, slots.at[slot(z_of(d), y, c)], y_send.at[d], y_recv.at[d], seq=slot(z, 1 - y, c))

    def to_c(side, d):
        index = slot(z_of(d), y if side == 0 else 1 - y, c)
        source = block if side == 0 and d == 0 else slots.at[index]
        return remote(source, slots.at[index], c_send.at[side, d], c_recv.at[side, d], seq=slot(z, y, 1 - c))

    local = pltpu.make_async_copy(block, slots.at[own], own_sem)
    ys = [to_y(d) for d in range(z_count)]
    cs = [[to_c(side, d) for d in range(z_count)] for side in range(2)]

    def start_z():
        local.start()
        for copy in to_z:
            copy.start()

    def relay(d):
        if d > 0:
            to_z[d - 1].wait_recv()
        ys[d].start()
        cs[0][d].start()

    def relay_across(d):
        ys[d].wait_recv()
        cs[1][d].start()

    def finish():
        for side in range(2):
            for d in range(z_count):
                cs[side][d].wait_recv()
        local.wait()

    def drain():
        for copy in to_z + ys + cs[0] + cs[1]:
            copy.wait_send()

    return start_z, relay, relay_across, finish, drain


def layer_kernel(
    seq_count, fsdp_count,
    sink_ref, span_ref, gain_ref, routing_ref,
    res_hbm, q_hbm, k_hbm, v_hbm, w_hbm, router_hbm, gate_hbm, up_hbm, down_hbm,
    attended_ref, layer_ref,
    res, q_raw, k_raw, v_raw, router, gate, up, down,
    kv_own, kv_all, w_own, w_all, q_rot, bias, rows_all, proj, got,
    x_out, arrived, stacked, back, returned, restacked,
    load_sems,
    kzs, kzr, kys, kyr, kcs, kcr, wzs, wzr, wys, wyr, wcs, wcr, own_sems, as_, ar, ps, pr,
    xs, xr, bs, br,
):
    sources = (k_hbm, v_hbm, w_hbm, q_hbm, res_hbm, router_hbm, gate_hbm, up_hbm, down_hbm)
    targets = (k_raw, v_raw, w_own, q_raw, res, router, gate, up, down)
    loads = [
        pltpu.make_async_copy(a, b, load_sems.at[i]) for i, (a, b) in enumerate(zip(sources, targets))
    ]
    for load in loads[:6]:
        load.start()

    me = lax.axis_index("seq")
    f_me = lax.axis_index("fsdp")
    z_count = seq_count // 4
    z, y, c = me // 4, lax.rem(me // 2, 2), lax.rem(me, 2)
    rows, key_count = bias.shape
    group_size = HEADS // KVH
    copies = seq_count // EXPERTS

    def spot(row):
        return jnp.where(row < HALF, span_ref[0, 2 * me], span_ref[0, 2 * me + 1]) * HALF + row % HALF

    lane = lax.broadcasted_iota(jnp.int32, (rows, 2 * HD), 1)
    place = spot(lax.broadcasted_iota(jnp.int32, (rows, 2 * HD), 0)).astype(jnp.float32)
    half = HD // 2
    frequency = jnp.exp(-jnp.log(rope_base) * (lane % half).astype(jnp.float32) / half)
    angles = place * frequency
    low = (lane % HD) < half
    cosine = jnp.cos(angles)
    sine = jnp.where(low, -jnp.sin(angles), jnp.sin(angles))

    def rotated(pair):
        x = pair.astype(jnp.float32)
        swapped = jnp.where(low, pltpu.roll(x, 2 * HD - half, 1), pltpu.roll(x, half, 1))
        return (x * cosine + swapped * sine).astype(jnp.bfloat16)

    loads[0].wait()
    loads[1].wait()
    for i in range(KVH // 2):
        kv_own[:, i * 2 * HD:(i + 1) * 2 * HD] = rotated(k_raw[:, i * 2 * HD:(i + 1) * 2 * HD])
    kv_own[:, KVH * HD:] = v_raw[...]

    def peer_of(side, dz, cc, sign=1):
        zz = lax.rem(z + dz, z_count) if sign > 0 else lax.rem(z + z_count - dz, z_count)
        return (zz * 2 + (1 - y if side else y)) * 2 + (1 - c if cc else c)

    relative = [(side, dz, cc) for side in range(2) for dz in range(z_count) for cc in range(2)]
    peers = [{"seq": peer_of(*r)} for r in relative[1:]]
    peers += [{"fsdp": lax.rem(f_me + d, fsdp_count)} for d in range(1, fsdp_count)]
    greet(peers)

    kv = gather_plan(kv_own, kv_all, (kzs, kzr, kys, kyr, kcs, kcr, own_sems.at[0]), z_count, z, y, c)
    w = gather_plan(w_own, w_all, (wzs, wzr, wys, wyr, wcs, wcr, own_sems.at[1]), z_count, z, y, c)
    kv[0]()
    kv[1](0)
    loads[2].wait()
    w[0]()
    loads[3].wait()
    for i in range(HEADS // 2):
        pair = rotated(q_raw[:, i * 2 * HD:(i + 1) * 2 * HD]) * jnp.bfloat16(HD ** -0.5)
        g, inside = (2 * i) // group_size, (2 * i) % group_size
        q_rot[g, inside * rows:(inside + 1) * rows, :] = pair[:, :HD]
        q_rot[g, (inside + 1) * rows:(inside + 2) * rows, :] = pair[:, HD:]
    key_row = lax.broadcasted_iota(jnp.int32, (1, key_count), 1)
    span_of_key = jnp.zeros((1, key_count), jnp.int32)
    for i in range(span_ref.shape[1]):
        span_of_key = jnp.where(key_row // HALF == i, span_ref[0, i], span_of_key)
    key_at = span_of_key * HALF + key_row % HALF
    query_at = spot(lax.broadcasted_iota(jnp.int32, (rows, 1), 0))
    bias[...] = jnp.where(key_at <= query_at, 0.0, masked_score)

    chosen = routing_ref[...]
    expert_lane = lax.broadcasted_iota(jnp.int32, (rows, EXPERTS), 1)
    picks = [chosen[:, j:j + 1] == expert_lane for j in range(TOPK)]
    named = sum(p.astype(jnp.float32) for p in picks)
    earlier = lax.broadcasted_iota(jnp.int32, (rows, rows), 1) < lax.broadcasted_iota(
        jnp.int32, (rows, rows), 0
    )
    before = jnp.dot(earlier.astype(jnp.float32), named, preferred_element_type=jnp.float32)
    slots = [
        jnp.sum(jnp.where(p, before, 0.0), axis=1, keepdims=True).astype(jnp.int32) for p in picks
    ]

    for d in range(1, z_count):
        kv[1](d)
    for d in range(z_count):
        kv[2](d)
    w[1](0)
    for load in loads[6:]:
        load.start()
    kv[3]()

    chunk = 4

    def send_rows(g):
        return [
            remote(
                rows_all.at[g, f_me], rows_all.at[g, f_me], as_.at[g, d], ar.at[g, d],
                fsdp=lax.rem(f_me + d, fsdp_count),
            )
            for d in range(1, fsdp_count)
        ]

    row_copies = [send_rows(g) for g in range(KVH)]
    relayed = 1
    for g in range(KVH):
        keys = kv_all[:, :, g * HD:(g + 1) * HD].reshape(key_count, HD)
        vals = kv_all[:, :, (KVH + g) * HD:(KVH + g + 1) * HD].reshape(key_count, HD)
        parts = []
        for part in range(group_size // chunk):
            q = q_rot[g, part * chunk * rows:(part + 1) * chunk * rows, :]
            s = lax.dot_general(q, keys, (((1,), (1,)), ((), ())), preferred_element_type=jnp.float32)
            weights, totals = [], []
            for i in range(chunk):
                sink = sink_ref[0, g * group_size + part * chunk + i]
                one = s[i * rows:(i + 1) * rows, :] + bias[...]
                top = jnp.maximum(jnp.max(one, axis=1, keepdims=True), sink)
                p = jnp.exp(one - top)
                totals.append(jnp.sum(p, axis=1, keepdims=True) + jnp.exp(sink - top))
                weights.append(p.astype(jnp.bfloat16))
            o = jnp.dot(jnp.concatenate(weights, axis=0), vals, preferred_element_type=jnp.float32)
            for i in range(chunk):
                parts.append((o[i * rows:(i + 1) * rows, :] / totals[i]).astype(jnp.bfloat16))
            if part == 0 and g > 0:
                for copy in row_copies[g - 1]:
                    copy.start()
        rows_all[g, pl.ds(f_me, 1)] = jnp.concatenate(parts, axis=1)[None]
        while relayed < z_count and relayed * KVH <= (g + 1) * z_count - KVH:
            w[1](relayed)
            relayed += 1
    for d in range(relayed, z_count):
        w[1](d)
    for copy in row_copies[KVH - 1]:
        copy.start()
    for d in range(z_count):
        w[2](d)
    loads[4].wait()
    loads[5].wait()
    w[3]()

    width = group_size * HD
    count = width // w_own.shape[0]
    total = None
    for g in range(KVH):
        for copy in row_copies[g]:
            copy.wait_recv()
        block = w_all[g * count:(g + 1) * count].reshape(width, w_own.shape[1])
        term = jnp.dot(
            rows_all[g].reshape(fsdp_count * rows, width), block, preferred_element_type=jnp.float32
        )
        total = term if total is None else total + term
    proj[...] = total.astype(jnp.bfloat16).reshape(proj.shape)
    backs = []
    for d in range(1, fsdp_count):
        peer = lax.rem(f_me + d, fsdp_count)
        backs.append(remote(proj.at[peer], got.at[f_me], ps.at[d], pr.at[d], fsdp=peer))
    for copy in backs:
        copy.start()
    got[pl.ds(f_me, 1)] = proj[pl.ds(f_me, 1)]
    kv[4]()
    w[4]()
    for g in range(KVH):
        for copy in row_copies[g]:
            copy.wait_send()
    for copy in backs:
        copy.wait_recv()
    columns = w_own.shape[1]
    for f in range(fsdp_count):
        attended_ref[:, f * columns:(f + 1) * columns] = got[f]
    for copy in backs:
        copy.wait_send()

    stream = res[...].astype(jnp.float32) + attended_ref[...].astype(jnp.float32)
    normed = (
        stream
        * lax.rsqrt(jnp.mean(stream * stream, axis=-1, keepdims=True) + norm_eps)
        * gain_ref[...].astype(jnp.float32)
    ).astype(jnp.bfloat16)
    place_lane = lax.broadcasted_iota(jnp.int32, (rows, EXPERTS * CAP), 1)
    dispatch = sum(
        (place_lane == chosen[:, j:j + 1] * CAP + slots[j]).astype(jnp.float32) for j in range(TOPK)
    ).astype(jnp.bfloat16)
    buffer = lax.dot_general(
        dispatch, normed, (((0,), (0,)), ((), ())), preferred_element_type=jnp.float32
    ).astype(jnp.bfloat16)
    for e in range(EXPERTS):
        x_out[e] = buffer[e * CAP:(e + 1) * CAP, :]

    sends, returns = {}, {}
    for r, rel in enumerate(relative[1:], 1):
        to, source = peer_of(*rel), peer_of(*rel, sign=-1)
        sends[r] = remote(x_out.at[to // copies], arrived.at[r], xs.at[r], xr.at[r], seq=to)
        returns[r] = remote(back.at[r], returned.at[me], bs.at[r], br.at[r], seq=source)
    own = pltpu.make_async_copy(x_out.at[me // copies], arrived.at[0], own_sems.at[2])
    keep = pltpu.make_async_copy(back.at[0], returned.at[me], own_sems.at[3])
    for copy in sends.values():
        copy.start()
    own.start()

    logits = jnp.dot(normed, router[...], preferred_element_type=jnp.float32)
    told = [jnp.sum(jnp.where(p, logits, 0.0), axis=1, keepdims=True) for p in picks]
    gates = [1.0 / sum(jnp.exp(t - told[j]) for t in told) for j in range(TOPK)]
    slot_lane = lax.broadcasted_iota(jnp.int32, (rows, seq_count * CAP), 1)
    mixing = sum(
        jnp.where(
            (slot_lane // (CAP * copies) == chosen[:, j:j + 1]) & (slot_lane % CAP == slots[j]),
            gates[j],
            0.0,
        )
        for j in range(TOPK)
    )
    coarse = mixing.astype(jnp.bfloat16)
    fine = (mixing - coarse.astype(jnp.float32)).astype(jnp.bfloat16)

    for load in loads[6:]:
        load.wait()
    per_side = len(relative) // 2
    for side in range(2):
        for i in range(per_side):
            r = side * per_side + i
            sends[r].wait_recv() if r > 0 else own.wait()
            stacked[i * CAP:(i + 1) * CAP, :] = arrived[r]
        x = stacked[...]
        g = jnp.dot(x, gate[...], preferred_element_type=jnp.float32)
        u = jnp.dot(x, up[...], preferred_element_type=jnp.float32)
        hidden = (g * jax.nn.sigmoid(1.702 * g) * (u + 1.0)).astype(jnp.bfloat16)
        part = jnp.dot(hidden, down[...], preferred_element_type=jnp.float32).astype(jnp.bfloat16)
        for i in range(per_side):
            back[side * per_side + i] = part[i * CAP:(i + 1) * CAP, :]
        for i in range(per_side):
            r = side * per_side + i
            returns[r].start() if r > 0 else keep.start()
    for copy in sends.values():
        copy.wait_send()
    for copy in returns.values():
        copy.wait_recv()
    keep.wait()
    for i in range(seq_count):
        restacked[i * CAP:(i + 1) * CAP, :] = returned[i]
    outs = restacked[...]
    mixed = jnp.dot(coarse, outs, preferred_element_type=jnp.float32) + jnp.dot(
        fine, outs, preferred_element_type=jnp.float32
    )
    layer_ref[...] = (
        res[...].astype(jnp.float32) + attended_ref[...].astype(jnp.float32) + mixed
    ).astype(jnp.bfloat16)
    for copy in returns.values():
        copy.wait_send()


def on_device(
    residual,
    queries,
    key_rows,
    values,
    attention_sinks,
    out_weight,
    norm_gain,
    router_weight,
    gate_weight,
    up_weight,
    down_weight,
    routing,
    span_order,
):
    seq_count = lax.axis_size("seq")
    fsdp_count = lax.axis_size("fsdp")
    z_count = seq_count // 4
    rows = residual.shape[1]
    dma = pltpu.SemaphoreType.DMA
    vmem = pl.BlockSpec(memory_space=pltpu.VMEM)
    smem = pl.BlockSpec(memory_space=pltpu.SMEM)
    hbm = pl.BlockSpec(memory_space=pl.ANY)
    gather_sems = [dma((z_count,))] * 4 + [dma((2, z_count))] * 2

    def held(*shape):
        return pltpu.VMEM(shape, jnp.bfloat16)

    kv_width = 2 * KVH * HD
    w_rows, columns = out_weight.shape
    attended, layer_output = pl.pallas_call(
        functools.partial(layer_kernel, seq_count, fsdp_count),
        out_shape=[jax.ShapeDtypeStruct((rows, D), jnp.bfloat16)] * 2,
        in_specs=[smem, smem, vmem, vmem] + [hbm] * 9,
        out_specs=[vmem, vmem],
        scratch_shapes=[
            held(rows, D),
            held(rows, HEADS * HD),
            held(rows, KVH * HD),
            held(rows, KVH * HD),
            held(*router_weight.shape),
            held(*gate_weight.shape),
            held(*up_weight.shape),
            held(*down_weight.shape),
            held(rows, kv_width),
            held(seq_count, rows, kv_width),
            held(w_rows, columns),
            held(seq_count, w_rows, columns),
            held(KVH, HEADS // KVH * rows, HD),
            pltpu.VMEM((rows, seq_count * rows), jnp.float32),
            held(KVH, fsdp_count, rows, HEADS // KVH * HD),
            held(fsdp_count, rows, columns),
            held(fsdp_count, rows, columns),
            held(EXPERTS, CAP, D),
            held(seq_count, CAP, D),
            held(seq_count // 2 * CAP, D),
            held(seq_count, CAP, D),
            held(seq_count, CAP, D),
            held(seq_count * CAP, D),
            dma((9,)),
        ]
        + gather_sems
        + gather_sems
        + [dma((4,)), dma((KVH, fsdp_count)), dma((KVH, fsdp_count)), dma((fsdp_count,)), dma((fsdp_count,))]
        + [dma((seq_count,))] * 4,
        compiler_params=pltpu.CompilerParams(
            collective_id=0, has_side_effects=True, vmem_limit_bytes=60 * 1024 * 1024
        ),
    )(
        attention_sinks[None, :],
        span_order[None, :],
        norm_gain[None, :],
        routing[0],
        residual[0],
        queries[0],
        key_rows[0],
        values[0],
        out_weight,
        router_weight,
        gate_weight,
        up_weight,
        down_weight,
    )
    return (attended[None], layer_output[None])


def solution(mesh):
    in_specs = (
        P("fsdp", "seq", None),
        P("fsdp", "seq", None),
        P("fsdp", "seq", None),
        P("fsdp", "seq", None),
        P(),
        P("seq", "fsdp"),
        P(),
        P(),
        P(None, "seq"),
        P(None, "seq"),
        P("seq", None),
        P("fsdp", "seq", None),
        P(),
    )
    out_specs = (P("fsdp", "seq", None), P("fsdp", "seq", None))
    return jax.shard_map(
        on_device, mesh=mesh, in_specs=in_specs, out_specs=out_specs, check_vma=False
    )
```
